32 devices in a mesh: diamond: 2 (over x), tile: 16 (over z, y, core).
Axes of the slice: x: 2, y: 2, z: 4, core: 2. Of those that a mesh axis runs over, the one named last changes fastest.
Arguments:
- inputs: bfloat16 [128, 64, 2048], P(None, 'diamond', 'tile'), may hold values from -6 to 6
- cotangent: bfloat16 [128, 64, 2048], P(None, 'diamond', 'tile'), may hold values from -6 to 6
- weight: bfloat16 [7, 128, 128], replicated, may hold values from -0.1875 to 0.1875
- bias: float32 [128], replicated, may hold values from -4 to 4
- ocean: int32 [4, 128], P('diamond', 'tile'), may hold values 0 or 1
Outputs:
- grad_inputs: bfloat16 [128, 64, 2048], P(None, 'diamond', 'tile')
- grad_weight: float32 [7, 128, 128], replicated
- grad_bias: float32 [128], replicated
The draws below stay inside these ranges and needn't reach their ends.
All inputs are finite; a program needn't handle non-finite values. No bound on the sum of `ocean` on one device may be relied on, other than what follows from the above.
Results may differ from the reference program's by a relative error of at most 0.005.
Values may be sent and summed in bfloat16 or wider, within the bound.
A program may use at most 128 MiB of HBM per device.

```python
import jax
import jax.numpy as jnp
from jax import lax

F = 128
BLOCK = 16
NR = 64
NC = 2048


def with_ends(array, rng, smallest, high):
    spot = [jax.random.randint(jax.random.fold_in(rng, axis), (), 0, length) for axis, length in enumerate(array.shape)]
    main_axis = array.shape.index(max(array.shape))
    beside = spot[:main_axis] + [(spot[main_axis] + 1) % array.shape[main_axis]] + spot[main_axis + 1:]
    return array.at[tuple(spot)].set(smallest).at[tuple(beside)].set(high)


def block_scale(own_key, shape, split, smallest, top_value):
    def one(axis_at, blocks):
        draws = jax.random.uniform(jax.random.fold_in(jax.random.fold_in(own_key, 6), axis_at), (blocks,), jnp.float32, smallest / len(split), top_value / len(split))
        return jnp.repeat(jnp.exp(draws), shape[axis_at] // blocks).reshape((-1,) + (1,) * (len(shape) - axis_at - 1))

    level = one(*split[0])
    for cut in split[1:]:
        level = level * one(*cut)
    return level


def normal_values(key, extent, spread, limit, cuts=(), kind=jnp.bfloat16):
    level = block_scale(key, extent, cuts, -0.22, 0.18) if cuts else 1.0
    array = jax.random.normal(key, extent, jnp.float32) * spread * level
    return jnp.minimum(jnp.maximum(array, -limit), limit).astype(kind)


def setup_inputs(seed: int = 0) -> dict:
    streams_of = jax.random.split(jax.random.key(seed), 6)
    return {
        "inputs": normal_values(streams_of[0], (F, NR, NC), 1.0, 6.0, ((1, 2), (2, 16))),
        "cotangent": normal_values(streams_of[1], (F, NR, NC), 1.0, 6.0, ((1, 2), (2, 16))),
        "weight": normal_values(streams_of[2], (7, F, F), (7 * F) ** -0.5, 0.1875),
        "bias": normal_values(streams_of[3], (F,), 1.0, 4.0, (), jnp.float32),
        "ocean": with_ends((jax.random.randint(streams_of[4], (NR // BLOCK, NC // BLOCK), 0, 4) < 3).astype(jnp.int32), jax.random.fold_in(streams_of[4], 1), 0, 1),
    }


OFFSETS = ((0, 0), (0, 1), (0, -1), (1, 0), (-1, 0), (1, -1), (-1, 1))


def stacked_taps(padded, rows, cols, sign):
    pieces = [padded[:, 1 + sign * dr:1 + sign * dr + rows, 1 + sign * dc:1 + sign * dc + cols] for dr, dc in OFFSETS]
    return jnp.stack(pieces, 0)


def reference(inputs, cotangent, weight, bias, ocean):
    feats, rows, cols = inputs.shape
    strip = 128 if cols % 128 == 0 else cols
    count = cols // strip
    cell_mask = jnp.repeat(jnp.repeat(ocean.astype(jnp.float32), BLOCK, 0), BLOCK, 1)
    scale = (rows * cols) ** -0.5
    x_pad = jnp.pad(inputs, ((0, 0), (1, 1), (1, 1)))
    flat_weight = weight.reshape(7 * feats, feats)

    def forward_strip(index):
        start = (index * strip).astype(jnp.int32)
        piece = lax.dynamic_slice_in_dim(x_pad, start, strip + 2, 2)
        taps = stacked_taps(piece, rows, strip, 1).reshape(7 * feats, rows * strip)
        pre = lax.dot_general(flat_weight, taps, (((0,), (0,)), ((), ())), preferred_element_type=jnp.float32) + bias[:, None]
        grad_piece = lax.dynamic_slice_in_dim(cotangent, start, strip, 2).reshape(feats, rows * strip).astype(jnp.float32)
        mask_piece = lax.dynamic_slice_in_dim(cell_mask, start, strip, 1).reshape(1, rows * strip)
        sig = jax.nn.sigmoid(pre)
        grad_pre = (mask_piece * grad_piece * sig * (1.0 + pre * (1.0 - sig))).astype(jnp.bfloat16)
        part_w = lax.dot_general(taps, grad_pre, (((1,), (1,)), ((), ())), preferred_element_type=jnp.float32)
        part_b = jnp.sum(grad_pre.astype(jnp.float32), axis=1)
        return grad_pre.reshape(feats, rows, strip), part_w, part_b

    grad_strips, parts_w, parts_b = lax.map(forward_strip, jnp.arange(count, dtype=jnp.int32))
    grad_pre = jnp.moveaxis(grad_strips, 0, 2).reshape(feats, rows, cols)
    grad_weight = (jnp.sum(parts_w, 0) * scale).reshape(7, feats, feats)
    grad_bias = jnp.sum(parts_b, 0) * scale
    g_pad = jnp.pad(grad_pre, ((0, 0), (1, 1), (1, 1)))
    back_weight = jnp.transpose(weight, (1, 0, 2)).reshape(feats, 7 * feats)

    def backward_strip(index):
        start = (index * strip).astype(jnp.int32)
        piece = lax.dynamic_slice_in_dim(g_pad, start, strip + 2, 2)
        taps = stacked_taps(piece, rows, strip, -1).reshape(7 * feats, rows * strip)
        total = jnp.dot(back_weight, taps, preferred_element_type=jnp.float32)
        own = lax.dynamic_slice_in_dim(cotangent, start, strip, 2).reshape(feats, rows * strip).astype(jnp.float32)
        return (own + total).astype(jnp.bfloat16).reshape(feats, rows, strip)

    dx_strips = lax.map(backward_strip, jnp.arange(count, dtype=jnp.int32))
    grad_inputs = jnp.moveaxis(dx_strips, 0, 2).reshape(feats, rows, cols)
    return grad_inputs, grad_weight, grad_bias
```

```python
import functools

import jax
import jax.numpy as jnp
from jax import lax
from jax.experimental import pallas as pl
from jax.experimental.pallas import tpu as pltpu
from jax.sharding import PartitionSpec as P

BLOCK = 16
LANES = 128
FORWARD = (1, 0, 2, 6, 4, 3, 5)
BACKWARD = (2, 0, 1, 5, 3, 4, 6)
MESH = pl.DeviceIdType.MESH
UP, DOWN, LEFT, RIGHT, UPRIGHT, LOWLEFT = range(6)
SUMMED = 32
f32, bf16 = jnp.float32, jnp.bfloat16


def kernel(D, T, R, F, summed, x_hbm, c_hbm, w_hbm, b_ref, m_ref, y_hbm, a_hbm,
           xv, cv, wv, xf, cf, xs, gs, wt, wb, bb, bacc, x_cols, g_cols, xh, gh,
           total, s1, r1, s2, r2, full, in_sem, xss, xrs, gss, grs, pair_sem, rs_s, rs_r, ag_s, ag_r):
    C = LANES
    d = lax.axis_index("diamond")
    t = lax.axis_index("tile")
    ins = [pltpu.make_async_copy(a, b, in_sem.at[i])
           for i, (a, b) in enumerate(((x_hbm, xv), (w_hbm, wv), (c_hbm, cv)))]
    for copy in ins:
        copy.start()

    up, down, left, right = d > 0, d < D - 1, t > 0, t < T - 1
    sends = (
        (down, (d + 1, t), UP, 1),
        (up, (d - 1, t), DOWN, 0),
        (right, (d, t + 1), LEFT, 3),
        (left, (d, t - 1), RIGHT, 2),
        (jnp.logical_and(down, left), (d + 1, t - 1), UPRIGHT, 2),
        (jnp.logical_and(up, right), (d - 1, t + 1), LOWLEFT, 3),
    )
    filled = (up, down, left, right, jnp.logical_and(up, right), jnp.logical_and(down, left))

    barrier = pltpu.get_barrier_semaphore()
    if summed:
        me = d * T + t
        for s in range(1, D * T):
            p = lax.rem(me + s, D * T)
            pl.semaphore_signal(barrier, inc=1, device_id=(p // T, p % T), device_id_type=MESH)
    else:
        for there, device, _, _ in sends:
            @pl.when(there)
            def _():
                pl.semaphore_signal(barrier, inc=1, device_id=device, device_id_type=MESH)

    lane = lax.broadcasted_iota(jnp.int32, (F, C), 1)

    def at(r):
        return pl.ds(pl.multiple_of(r * C, C), C)

    def spread(source, target):
        @pl.loop(0, F // 8)
        def _(i):
            f = pl.multiple_of(i * 8, 8)
            target[pl.ds(pl.multiple_of(i * 8 * R, 8 * R), 8 * R), :] = (
                source[pl.ds(f, 8)].reshape(8 * R, C).astype(f32))

    def columns(value, r, cols):
        cols[0] = jnp.where(lane == r, pltpu.roll(value, r, 1), cols[0])
        cols[1] = jnp.where(lane == r, pltpu.roll(value, r + 1, 1), cols[1])

    def halo_copies(stack, edge, halo, ssem, rsem):
        pieces = (stack.at[F:2 * F, C:2 * C], stack.at[F:2 * F, R * C:(R + 1) * C], edge.at[0], edge.at[1])
        return [(there, pltpu.make_async_remote_copy(
            src_ref=pieces[piece], dst_ref=halo.at[slot], send_sem=ssem.at[slot], recv_sem=rsem.at[slot],
            device_id=device, device_id_type=MESH)) for there, device, slot, piece in sends]

    def start(copies):
        for there, copy in copies:
            @pl.when(there)
            def _():
                copy.start()

    def finish(copies, stack, halo):
        for there, copy in copies:
            @pl.when(there)
            def _():
                copy.wait_send()
        for slot in range(6):
            @pl.when(filled[slot])
            def _():
                copies[slot][1].wait_recv()

            @pl.when(jnp.logical_not(filled[slot]))
            def _():
                halo[slot] = jnp.zeros((F, C), bf16)
        above, below = halo[UP], halo[DOWN]
        stack[F:2 * F, 0:C] = above
        stack[F:2 * F, (R + 1) * C:(R + 2) * C] = below
        corner = pltpu.roll(halo[UPRIGHT].astype(f32), C - R, 1)
        stack[0:F, 0:C] = jnp.where(lane == C - 1, corner, pltpu.roll(above.astype(f32), C - 1, 1)).astype(bf16)
        corner = halo[LOWLEFT].astype(f32)
        stack[2 * F:3 * F, (R + 1) * C:(R + 2) * C] = jnp.where(
            lane == 0, corner, pltpu.roll(below.astype(f32), 1, 1)).astype(bf16)

        @pl.loop(0, R)
        def _(r):
            value = stack[F:2 * F, at(r + 1)].astype(f32)
            after = pltpu.roll(halo[RIGHT].astype(f32), C - 1 - r, 1)
            before = pltpu.roll(halo[LEFT].astype(f32), lax.rem(C - r, C), 1)
            stack[0:F, at(r + 1)] = jnp.where(lane == C - 1, after, pltpu.roll(value, C - 1, 1)).astype(bf16)
            stack[2 * F:3 * F, at(r + 1)] = jnp.where(lane == 0, before, pltpu.roll(value, 1, 1)).astype(bf16)

    def conv(weights, stack, r, rows):
        def some(r):
            return pl.ds(pl.multiple_of(r * C, C), rows * C)
        out = jnp.dot(weights[:, 0:3 * F], stack[:, some(r + 1)], preferred_element_type=f32)
        out += jnp.dot(weights[:, 3 * F:5 * F], stack[0:2 * F, some(r)], preferred_element_type=f32)
        return out + jnp.dot(weights[:, 5 * F:7 * F], stack[F:3 * F, some(r + 2)], preferred_element_type=f32)

    ins[0].wait()
    spread(xv, xf)

    @pl.loop(0, R)
    def _(r):
        value = xf[pl.ds(r, F, stride=R), :]
        xs[F:2 * F, at(r + 1)] = value.astype(bf16)
        columns(value, r, x_cols[0])

    x_cols[1][...] = x_cols[0][...].astype(bf16)
    if summed:
        pl.semaphore_wait(barrier, D * T - 1)
    else:
        for there in filled:
            @pl.when(there)
            def _():
                pl.semaphore_wait(barrier, 1)
    x_copies = halo_copies(xs, x_cols[1], xh, xss, xrs)
    start(x_copies)

    ins[1].wait()
    for slot, (k, j) in enumerate(zip(FORWARD, BACKWARD)):
        wt[:, slot * F:(slot + 1) * F] = wv[k].astype(f32).T.astype(bf16)
        wb[:, slot * F:(slot + 1) * F] = wv[j]
    bb[...] = jnp.broadcast_to(b_ref[...], (F, F)).T
    bacc[...] = jnp.zeros_like(bacc)
    ins[2].wait()
    spread(cv, cf)
    finish(x_copies, xs, xh)

    step = 4

    @pl.loop(0, R // step)
    def _(i):
        pre = conv(wt, xs, i * step, step)
        mask = m_ref[pl.ds(i * step // BLOCK, 1), :]
        for j in range(step):
            r = i * step + j
            z = pre[:, j * C:(j + 1) * C] + bb[...]
            s = 0.5 + 0.5 * jnp.tanh(0.5 * z)
            g = (mask * cf[pl.ds(r, F, stride=R), :] * s * (1.0 + z * (1.0 - s))).astype(bf16)
            gs[F:2 * F, at(r + 1)] = g
            g = g.astype(f32)
            bacc[...] += g
            columns(g, r, g_cols[0])

    g_cols[1][...] = g_cols[0][...].astype(bf16)
    g_copies = halo_copies(gs, g_cols[1], gh, gss, grs)
    start(g_copies)

    wide = 8
    total[...] = jnp.zeros_like(total)

    @pl.loop(0, R // wide)
    def _(i):
        def some(r):
            return pl.ds(pl.multiple_of(r * C, C), wide * C)
        r = i * wide
        g = gs[F:2 * F, some(r + 1)]
        for first, many, rows, row in ((0, 3, slice(0, 3 * F), r + 1), (3, 2, slice(0, 2 * F), r), (5, 2, slice(F, 3 * F), r + 2)):
            part = lax.dot_general(xs[rows, some(row)], g, (((1,), (1,)), ((), ())), preferred_element_type=f32)
            for j in range(many):
                k = FORWARD[first + j]
                total[k * F:(k + 1) * F, :] += part[j * F:(j + 1) * F, :]

    total[7 * F:8 * F, :] = jnp.broadcast_to(jnp.sum(bacc[...].T, axis=0, keepdims=True), (F, F))

    def back(first, last):
        @pl.loop(first, last)
        def _(i):
            part = conv(wb, gs, i * step, step)
            for j in range(step):
                r = i * step + j
                xf[pl.ds(r, F, stride=R), :] = part[:, j * C:(j + 1) * C] + cf[pl.ds(r, F, stride=R), :]

    def put():
        @pl.loop(0, F // 8)
        def _(i):
            f = pl.multiple_of(i * 8, 8)
            xv[pl.ds(f, 8)] = xf[pl.ds(pl.multiple_of(i * 8 * R, 8 * R), 8 * R), :].astype(bf16).reshape(8, R, C)
        copy = pltpu.make_async_copy(xv, y_hbm, in_sem.at[0])
        copy.start()
        return copy

    if not summed:
        finish(g_copies, gs, gh)
        back(0, R // step)
        y_copy = put()
        a_copy = pltpu.make_async_copy(total, a_hbm, in_sem.at[1])
        a_copy.start()
        a_copy.wait()
        y_copy.wait()
        return

    pairs = D * T // 2
    core = t % 2
    own = d * (T // 2) + t // 2
    half = 8 * F // 2
    piece = half // pairs
    partner = (d, t + 1 - 2 * core)
    theirs = pl.ds(pl.multiple_of((1 - core) * half, half), half)
    mine = pl.ds(pl.multiple_of(core * half, half), half)
    s1[...] = total[theirs, :].astype(bf16)
    first = pltpu.make_async_remote_copy(
        src_ref=s1, dst_ref=r1, send_sem=pair_sem.at[0], recv_sem=pair_sem.at[1],
        device_id=partner, device_id_type=MESH)
    first.start()
    finish(g_copies, gs, gh)
    first.wait()
    s2[...] = (total[mine, :] + r1[...].astype(f32)).astype(bf16)

    def other(s):
        p = lax.rem(own + s, pairs)
        return p, (p // (T // 2), 2 * (p % (T // 2)) + core)

    def rows_of(p):
        return pl.ds(pl.multiple_of(p * piece, piece), piece)

    scatters = []
    for s in range(1, pairs):
        p, device = other(s)
        copy = pltpu.make_async_remote_copy(
            src_ref=s2.at[rows_of(p)], dst_ref=r2.at[own], send_sem=rs_s.at[s], recv_sem=rs_r.at[own],
            device_id=device, device_id_type=MESH)
        copy.start()
        scatters.append(copy)
    r2[own] = s2[rows_of(own), :]
    back(0, R // step)
    y_copy = put()

    for s in range(1, pairs):
        p, device = other(s)
        pltpu.make_async_remote_copy(
            src_ref=s2.at[rows_of(p)], dst_ref=r2.at[p], send_sem=rs_s.at[s], recv_sem=rs_r.at[p],
            device_id=device, device_id_type=MESH).wait_recv()
    ended = r2[0].astype(f32)
    for p in range(1, pairs):
        ended += r2[p].astype(f32)

    def place(p):
        return full.at[pl.ds(pl.multiple_of(core * half + p * piece, piece), piece)]

    full[pl.ds(pl.multiple_of(core * half + own * piece, piece), piece), :] = ended.astype(bf16)
    gathers = []
    for s in range(1, pairs):
        p, device = other(s)
        copy = pltpu.make_async_remote_copy(
            src_ref=place(own), dst_ref=place(own), send_sem=ag_s.at[s], recv_sem=ag_r.at[own],
            device_id=device, device_id_type=MESH)
        copy.start()
        gathers.append(copy)
    for s in range(1, pairs):
        p, device = other(s)
        pltpu.make_async_remote_copy(
            src_ref=place(own), dst_ref=place(p), send_sem=ag_s.at[s], recv_sem=ag_r.at[p],
            device_id=device, device_id_type=MESH).wait_recv()
    last = pltpu.make_async_remote_copy(
        src_ref=full.at[mine], dst_ref=full.at[mine], send_sem=pair_sem.at[2], recv_sem=pair_sem.at[3],
        device_id=partner, device_id_type=MESH)
    last.start()
    for copy in scatters + gathers:
        copy.wait_send()
    last.wait()
    a_copy = pltpu.make_async_copy(full, a_hbm, in_sem.at[1])
    a_copy.start()
    a_copy.wait()
    y_copy.wait()


def on_device(D, T, inputs, cotangent, weight, bias, ocean):
    F, R, C = inputs.shape
    assert C == LANES and F == LANES
    summed = D * T <= SUMMED
    pairs = D * T // 2 if summed else 1
    piece = 4 * F // pairs
    scale = (R * C * D * T) ** -0.5
    mask = jnp.repeat(ocean.astype(f32), BLOCK, 1)
    any_space = pl.BlockSpec(memory_space=pl.ANY)
    vmem = pl.BlockSpec(memory_space=pltpu.VMEM)
    dma = pltpu.SemaphoreType.DMA
    grad_inputs, sums = pl.pallas_call(
        functools.partial(kernel, D, T, R, F, summed),
        out_shape=(
            jax.ShapeDtypeStruct((F, R, C), bf16),
            jax.ShapeDtypeStruct((8 * F, F), bf16 if summed else f32),
        ),
        in_specs=[any_space, any_space, any_space, vmem, vmem],
        out_specs=(any_space, any_space),
        scratch_shapes=[
            pltpu.VMEM((F, R, C), bf16), pltpu.VMEM((F, R, C), bf16), pltpu.VMEM((7, F, F), bf16),
            pltpu.VMEM((F * R, C), f32), pltpu.VMEM((F * R, C), f32),
            pltpu.VMEM((3 * F, (R + 2) * C), bf16), pltpu.VMEM((3 * F, (R + 2) * C), bf16),
            pltpu.VMEM((F, 7 * F), bf16), pltpu.VMEM((F, 7 * F), bf16),
            pltpu.VMEM((F, F), f32), pltpu.VMEM((F, C), f32),
            [pltpu.VMEM((2, F, C), f32), pltpu.VMEM((2, F, C), bf16)],
            [pltpu.VMEM((2, F, C), f32), pltpu.VMEM((2, F, C), bf16)],
            pltpu.VMEM((6, F, C), bf16), pltpu.VMEM((6, F, C), bf16),
            pltpu.VMEM((8 * F, F), f32), pltpu.VMEM((4 * F, F), bf16), pltpu.VMEM((4 * F, F), bf16),
            pltpu.VMEM((4 * F, F), bf16), pltpu.VMEM((pairs, piece, F), bf16), pltpu.VMEM((8 * F, F), bf16),
            dma((3,)), dma((6,)), dma((6,)), dma((6,)), dma((6,)), dma((4,)),
            dma((pairs,)), dma((pairs,)), dma((pairs,)), dma((pairs,)),
        ],
        compiler_params=pltpu.CompilerParams(collective_id=0, has_side_effects=True),
        name="hex_backward",
    )(inputs, cotangent, weight, bias.reshape(1, F), mask)
    if not summed:
        sums = lax.psum(sums, ("diamond", "tile"))
    sums = sums.astype(f32) * scale
    return grad_inputs, sums[:7 * F].reshape(7, F, F), sums[7 * F]


def solution(mesh):
    cells = P(None, "diamond", "tile")
    return jax.shard_map(
        functools.partial(on_device, mesh.shape["diamond"], mesh.shape["tile"]),
        mesh=mesh,
        in_specs=(cells, cells, P(), P(), P("diamond", "tile")),
        out_specs=(cells, P(), P()),
        check_vma=False,
    )
```
